32 devices in a mesh: runs: 2 (over y), row: 4 (over z), col: 2 (over x), sub: 2 (over core).
Axes of the slice: x: 2, y: 2, z: 4, core: 2. Of those that a mesh axis runs over, the one named last changes fastest.
Arguments:
- packed: bfloat16 [4, 2048, 256], P(('col', 'sub'), ('runs', 'row')), parts along dimension 1, may hold values from -6 to 6
- h_real: bfloat16 [8, 4, 128, 128], P('row'), may hold values from -0.25 to 0.25
- h_imag: bfloat16 [8, 4, 128, 128], P('row'), may hold values from -0.25 to 0.25
- h_cols: int32 [8, 4], P('row'), may hold values from 0 to 7, as said below
Outputs:
- evolved: float32 [4, 2048, 256], P(('col', 'sub'), ('runs', 'row')), parts along dimension 1
The draws below stay inside these ranges and needn't reach their ends.
There are 2 independent parts, one for each index of `runs`. The reference program is written for one: setup_inputs(seed, part) draws one part's arguments, and reference() takes and returns one part's arrays. A program takes and returns all parts, laid end to end along the dimension named above; an argument that names none is the same for every part. Nothing has to cross between parts.
Inputs may be any that keep to these rules, and one draw needn't show every extreme that they name: h_cols[b, 0] = b, and h_cols[b, 1], h_cols[b, 2], h_cols[b, 3] are (b + e) mod 8 for three different e among -2, -1, 1, 2.
All inputs are finite; a program needn't handle non-finite values.
Results may differ from the reference program's by a relative error of at most 0.0027.
Values may be sent and summed in bfloat16 or wider, within the bound.
A program may use at most 64 MiB of HBM per device.

```python
import jax
import jax.numpy as jnp
from jax import lax

BLOCK = 128
TERMS = 3
PIECES = 4
PIECE = 64
BANDS = 4
ORDER = 1024
NBLOCKS = 8


def draw_h_cols(key, part):
    block_rows = jnp.arange(NBLOCKS, dtype=jnp.int32)
    dropped = jax.random.randint(key, (NBLOCKS,), 0, 4).astype(jnp.int32)
    offset_list = jnp.array([-2, -1, 1, 2], dtype=jnp.int32)
    slot_index = jnp.arange(3, dtype=jnp.int32)
    chosen = slot_index[None, :] + (slot_index[None, :] >= dropped[:, None]).astype(jnp.int32)
    kept_offsets = offset_list[chosen]
    offsets = jnp.concatenate([jnp.zeros((NBLOCKS, 1), jnp.int32), kept_offsets], axis=1)
    return ((block_rows[:, None] + offsets) % NBLOCKS).astype(jnp.int32)


def shard_levels(own_key, dims, shards, least, top_value):
    factor_of = 1.0
    for dim, parts in shards:
        draws = jax.random.uniform(jax.random.fold_in(jax.random.fold_in(own_key, 6), dim), (parts,), jnp.float32, least / len(shards), top_value / len(shards))
        factor_of = factor_of * jnp.repeat(jnp.exp(draws), dims[dim] // parts).reshape((-1,) + (1,) * (len(dims) - 1 - dim))
    return factor_of


def bell_draw(stream_key, dims, width, most, shards=(), kind=jnp.bfloat16):
    values = jax.random.normal(stream_key, dims, jnp.float32) * width
    if len(shards) > 0:
        values = shard_levels(stream_key, dims, shards, -0.22, 0.18) * values
    return jnp.clip(values, min=-most, max=most).astype(kind)


def setup_inputs(seed: int = 0, part: int = 0) -> dict:
    key_list = jax.random.split(jax.random.key(seed), 5)
    part_keys = jax.random.split(jax.random.fold_in(key_list[4], part), 5)
    return {
        "packed": bell_draw(part_keys[0], (PIECES, ORDER, BANDS * PIECE), 1.0, 6.0, ((0, 4), (1, 4))),
        "h_real": bell_draw(key_list[1], (NBLOCKS, 4, BLOCK, BLOCK), (4 * BLOCK) ** -0.5, 0.25, ((0, 4),)),
        "h_imag": bell_draw(key_list[2], (NBLOCKS, 4, BLOCK, BLOCK), (4 * BLOCK) ** -0.5, 0.25, ((0, 4),)),
        "h_cols": draw_h_cols(jax.random.fold_in(key_list[4], 71), part),
    }


step_size = 0.5


def unpack(packed):
    grid = packed.reshape(PIECES, ORDER, BANDS, PIECE)
    return jnp.transpose(grid, (1, 2, 0, 3)).reshape(ORDER, ORDER)


def pack_back(matrix):
    grid = matrix.reshape(ORDER, BANDS, PIECES, PIECE)
    return jnp.transpose(grid, (2, 0, 1, 3)).reshape(PIECES, ORDER, BANDS * PIECE)


def reference(packed, h_real, h_imag, h_cols):
    full = unpack(packed)
    mirrored = full.T
    row_ids = jnp.arange(ORDER, dtype=jnp.int32)[:, None]
    col_ids = jnp.arange(ORDER, dtype=jnp.int32)[None, :]
    upper_mask = row_ids <= col_ids
    real_part = jnp.where(upper_mask, full, mirrored)
    imag_part = jnp.where(row_ids > col_ids, full, jnp.where(row_ids < col_ids, -mirrored, jnp.zeros_like(mirrored)))
    current = jnp.stack([real_part, imag_part])
    summed = current.astype(jnp.float32)
    weights = jnp.stack([h_real, h_imag])
    for term_index in range(1, TERMS + 1):
        def one_row(block_row, current=current):
            col_blocks = h_cols[block_row]
            pieces = jax.vmap(lambda column: lax.dynamic_slice_in_dim(current, (column * BLOCK).astype(jnp.int32), BLOCK, 1))(col_blocks)
            row_weights = lax.dynamic_index_in_dim(weights, block_row, 1, keepdims=False)
            product = jnp.einsum("hsij,sgjc->hgic", row_weights.astype(jnp.float32), pieces.astype(jnp.float32))
            real_gen = product[0, 1] + product[1, 0]
            imag_gen = product[1, 1] - product[0, 0]
            return jnp.stack([real_gen, imag_gen]).astype(jnp.bfloat16)

        rows_out = lax.map(one_row, jnp.arange(NBLOCKS, dtype=jnp.int32))
        generator = jnp.transpose(rows_out, (1, 0, 2, 3)).reshape(2, ORDER, ORDER)
        as_float = generator.astype(jnp.float32)
        flipped = jnp.swapaxes(as_float, 1, 2)
        update = (step_size / term_index) * jnp.stack([as_float[0] + flipped[0], as_float[1] - flipped[1]])
        summed = summed + update
        current = update.astype(jnp.bfloat16)
    return pack_back(jnp.where(upper_mask, summed[0], summed[1]))
```

```python
import functools

import jax
import jax.numpy as jnp
from jax import lax
from jax.experimental import pallas as pl
from jax.experimental.pallas import tpu as pltpu
from jax.sharding import PartitionSpec as P

TERMS = 3


step_size = 0.5


def extended(block, sides, width):
    for axis, dim in sides:
        count = lax.axis_size(axis)
        forward = [(i, i + 1) for i in range(count - 1)]
        forward.append((count - 1, 0))
        backward = [(target, source) for source, target in forward]
        low = lax.ppermute(
            lax.slice_in_dim(block, block.shape[dim] - width, None, axis=dim), axis, forward
        )
        high = lax.ppermute(lax.slice_in_dim(block, 0, width, axis=dim), axis, backward)
        block = jnp.concatenate([low, block, high], axis=dim)
    return block


def mirror(stacked):
    groups, rows_here, col_count = stacked.shape
    piece_count = lax.axis_size(("col", "sub"))
    band_count = lax.axis_size("row")
    piece_len = rows_here // piece_count
    split_rows = stacked.reshape(groups, piece_count, piece_len, col_count)
    arrived = lax.all_to_all(split_rows, ("col", "sub"), split_axis=1, concat_axis=1, tiled=True)
    turned = jnp.swapaxes(arrived.reshape(groups, rows_here, col_count), 1, 2).reshape(
        groups, band_count, piece_len, rows_here
    )
    landed = lax.all_to_all(turned, "row", split_axis=1, concat_axis=1, tiled=True)
    spread = landed.reshape(groups, band_count, piece_len, piece_count, piece_len)
    placed = jnp.transpose(spread, (0, 3, 2, 1, 4))
    return placed.reshape(groups, rows_here, col_count)


def body(packed, h_real, h_imag, h_cols):
    packed_here = packed.reshape(packed.shape[1], packed.shape[2])
    rows_here, col_count = packed_here.shape
    band_index = lax.axis_index("row")
    piece_index = lax.axis_index(("col", "sub"))
    piece_len = rows_here // lax.axis_size(("col", "sub"))
    flipped = mirror(packed_here[None])[0]
    row_ids = band_index * rows_here + jnp.arange(rows_here, dtype=jnp.int32)[:, None]
    col_local = jnp.arange(col_count, dtype=jnp.int32)[None, :]
    col_ids = col_local // piece_len * rows_here + piece_index * piece_len + col_local % piece_len
    upper_mask = row_ids <= col_ids
    real_part = jnp.where(upper_mask, packed_here, flipped)
    imag_part = jnp.where(
        row_ids > col_ids,
        packed_here,
        jnp.where(row_ids < col_ids, -flipped, jnp.zeros_like(flipped)),
    )
    current = jnp.stack([real_part, imag_part])
    summed = current.astype(jnp.float32)
    combined = jnp.stack([jnp.stack([h_imag, h_real], 2), jnp.stack([-h_real, h_imag], 2)])
    local_blocks = h_real.shape[0]
    block_len = h_real.shape[2]
    block_total = lax.axis_size("row") * local_blocks
    block_ids = band_index * local_blocks + jnp.arange(local_blocks, dtype=jnp.int32)[:, None]
    offsets = (h_cols - block_ids + 2) % block_total - 2
    starts = (
        (jnp.arange(local_blocks, dtype=jnp.int32)[:, None] + offsets + 2) * block_len
    ).reshape(-1)
    for term_index in range(1, TERMS + 1):
        padded = extended(current, (("row", 1),), 2 * block_len)
        sliced = jax.vmap(
            lambda row_start: lax.dynamic_slice_in_dim(padded, row_start, block_len, 1)
        )(starts)
        gathered = sliced.reshape(local_blocks, 4, 2, block_len, col_count)
        product = jnp.einsum(
            "obsgij,bsgjc->obic", combined, gathered, preferred_element_type=jnp.float32
        )
        generator = product.reshape(2, rows_here, col_count).astype(jnp.bfloat16)
        mirror_part = mirror(generator).astype(jnp.float32)
        own_part = generator.astype(jnp.float32)
        update = (
            step_size
            / term_index
            * jnp.stack([own_part[0] + mirror_part[0], own_part[1] - mirror_part[1]])
        )
        summed = summed + update
        current = update.astype(jnp.bfloat16)
    result = jnp.where(upper_mask, summed[0], summed[1])
    return result[None]


MESH_ID = pl.DeviceIdType.MESH


def gather_kernel(
    sizes, packed_ref, h_real_ref, h_imag_ref, cols_ref, out_ref,
    whole, blocks, cols_vmem, cols_smem, current, generator,
    local_sem, send_sem, relay_sem, recv_sem, h_send, h_relay, h_recv, cols_send, cols_recv,
):
    bands, pieces, piece_len, block_len, local_blocks, slots = sizes
    rows_here = pieces * piece_len
    width = bands * piece_len
    order = bands * rows_here
    per_block = block_len // piece_len
    strip = 2 * piece_len
    z = lax.axis_index("row")
    x = lax.axis_index("col")
    s = lax.axis_index("sub")
    y = lax.axis_index("runs")
    piece = x * 2 + s
    x_peer, s_peer, y_peer = {"col": 1 - x}, {"sub": 1 - s}, {"runs": 1 - y}

    halves = 2
    half = pieces // halves

    def spot(band, owner, part):
        start = pl.multiple_of(owner * width, width)
        return whole.at[pl.ds(part * half, half), band, :, pl.ds(start, width)]

    def nearest(position):
        inner = jnp.minimum(z, bands - 1 - z)
        sign = 1 if position % 2 == 0 else -1
        beyond = jnp.where(z < bands - 1 - z, z + (position - inner), z - (position - inner))
        return jnp.where(position <= 2 * inner, z + sign * ((position + 1) // 2), beyond)

    others = [nearest(position) for position in range(1, bands)]
    loads = [
        pltpu.make_async_copy(
            packed_ref.at[pl.ds(part * half, half)], spot(z, piece, part), local_sem.at[part]
        )
        for part in range(halves)
    ]
    loads += [
        pltpu.make_async_copy(h_real_ref, blocks.at[0, z], local_sem.at[2]),
        pltpu.make_async_copy(h_imag_ref, blocks.at[1, z], local_sem.at[3]),
        pltpu.make_async_copy(cols_ref, cols_vmem.at[z], local_sem.at[4]),
    ]
    for load in loads:
        load.start()
    barrier = pltpu.get_barrier_semaphore()
    up, down = {"row": lax.rem(z + 1, bands)}, {"row": lax.rem(z + bands - 1, bands)}
    has_up, has_down = z < bands - 1, z > 0

    def greet(peer):
        pl.semaphore_signal(barrier, 1, device_id=peer, device_id_type=MESH_ID)

    for peer in (s_peer, x_peer, y_peer):
        greet(peer)
    pl.when(has_up)(lambda: greet(up))
    pl.when(has_down)(lambda: greet(down))
    inside = jnp.logical_and(has_up, has_down)
    pl.semaphore_wait(barrier, 3 + jnp.where(inside, 2, 1))

    def send_packed(band, owner, part, sender, peer):
        return pltpu.make_async_remote_copy(
            src_ref=spot(band, owner, part), dst_ref=spot(band, owner, part), send_sem=sender,
            recv_sem=recv_sem.at[band, owner, part], device_id=peer, device_id_type=MESH_ID,
        )

    h_half = slots

    def send_h(kind, band, row, part, sender, peer):
        place = blocks.at[kind, band, row, pl.ds(part * h_half, h_half)]
        return pltpu.make_async_remote_copy(
            src_ref=place, dst_ref=place, send_sem=sender,
            recv_sem=h_recv.at[kind, band, row, part], device_id=peer, device_id_type=MESH_ID,
        )

    def send_cols(band, sender, peer):
        return pltpu.make_async_remote_copy(
            src_ref=cols_vmem.at[band], dst_ref=cols_vmem.at[band], send_sem=sender,
            recv_sem=cols_recv.at[band], device_id=peer, device_id_type=MESH_ID,
        )

    def cols_up(band, part):
        return send_cols(band, cols_send.at[0, band], up)

    def cols_down(band, part):
        return send_cols(band, cols_send.at[1, band], down)

    def no_side(band, part):
        return []

    def packed_up(band, part):
        return send_packed(band, piece, part, send_sem.at[0, band, part], up)

    def packed_down(band, part):
        return send_packed(band, piece, part, send_sem.at[1, band, part], down)

    def packed_side(band, part):
        return [send_packed(band, piece, part, send_sem.at[2, band, part], x_peer),
                send_packed(band, piece, part, send_sem.at[3, band, part], s_peer)]

    def packed_across(band, part):
        return send_packed(band, (1 - x) * 2 + s, part, relay_sem.at[band, part], s_peer)

    def h_up(band, part):
        return send_h(y, band, s, part, h_send.at[0, band, part], up)

    def h_down(band, part):
        return send_h(y, band, s, part, h_send.at[1, band, part], down)

    def h_side(band, part):
        return [send_h(y, band, s, part, h_send.at[2, band, part], y_peer),
                send_h(y, band, s, part, h_send.at[3, band, part], s_peer)]

    def h_across(band, part):
        return send_h(1 - y, band, s, part, h_relay.at[band, part], s_peer)

    def start_all(copies):
        for copy in copies:
            copy.start()

    def pass_on(copy):
        copy.wait_recv()
        copy.start()

    for part in range(halves):
        loads[part].wait()
        pl.when(has_up)(lambda: packed_up(z, part).start())
        pl.when(has_down)(lambda: packed_down(z, part).start())
        start_all(packed_side(z, part))
    for load in loads[halves:]:
        load.wait()
    pl.when(has_up)(lambda: cols_up(z, 0).start())
    pl.when(has_down)(lambda: cols_down(z, 0).start())
    pl.when(has_up)(lambda: h_up(z, 0).start())
    pl.when(has_down)(lambda: h_down(z, 0).start())

    def relay_step(step, make_up, make_down, make_side, count):
        below, above = z - step, z + step
        for part in range(count):
            @pl.when(below >= 0)
            def _():
                make_up(below, part).wait_recv()
                pl.when(has_up)(lambda: make_up(below, part).start())
                start_all(make_side(below, part))

            @pl.when(above < bands)
            def _():
                make_down(above, part).wait_recv()
                pl.when(has_down)(lambda: make_down(above, part).start())
                start_all(make_side(above, part))

    def cross_step(step, make_across, count):
        for part in range(count):
            pl.when(z - step >= 0)(lambda: pass_on(make_across(z - step, part)))
            pl.when(z + step < bands)(lambda: pass_on(make_across(z + step, part)))

    def h_ready(position):
        for kind in range(2):
            for part in range(1):
                send_h(
                    kind, others[position], 1 - s, part, h_relay.at[0, 0], s_peer
                ).wait_recv()

    for step in range(1, bands):
        relay_step(step, packed_up, packed_down, packed_side, halves)
        if step == 1:
            for part in range(halves):
                pass_on(packed_across(z, part))
        else:
            cross_step(step - 1, packed_across, halves)
            relay_step(step - 1, cols_up, cols_down, no_side, 1)
        if step == 2:
            relay_step(step - 1, h_up, h_down, h_side, 1)
    cross_step(bands - 1, packed_across, halves)
    relay_step(bands - 1, cols_up, cols_down, no_side, 1)
    cross_step(1, h_across, 1)
    for step in range(2, bands - 1):
        relay_step(step, h_up, h_down, h_side, 1)
    for band in range(bands):
        for owner in (x * 2 + (1 - s), (1 - x) * 2 + (1 - s)):
            for part in range(halves):
                send_packed(band, owner, part, relay_sem.at[band, part], s_peer).wait_recv()

    def column_ids(count):
        place = lax.broadcasted_iota(jnp.int32, (1, count), 1)
        return place

    def natural(place):
        owner = place // width
        within = place - owner * width
        band = within // piece_len
        return band * rows_here + owner * piece_len + within - band * piece_len

    def turned(ref, start):
        tall = ref[:, :, :, pl.ds(start, strip)].reshape(order, strip)
        return jnp.transpose(tall)

    strips_per_piece = bands // 2

    def unpack(index, carry):
        start = pl.multiple_of(index * strip, strip)
        owner, band = index // strips_per_piece, index % strips_per_piece * 2
        here = whole[owner, pl.ds(band, 2)].reshape(strip, order)
        flipped = turned(whole, start)
        row_ids = natural(index * strip + lax.broadcasted_iota(jnp.int32, (strip, 1), 0))
        col_ids = natural(column_ids(order))
        here = here.astype(jnp.float32)
        flipped = flipped.astype(jnp.float32)
        gap = row_ids - col_ids
        real_part = jnp.where(gap <= 0, here, flipped)
        imag_part = jnp.where(gap > 0, here, jnp.where(gap < 0, -flipped, 0.0))
        shape = (2, piece_len, order)
        current[0, owner, pl.ds(band, 2)] = real_part.astype(jnp.bfloat16).reshape(shape)
        current[1, owner, pl.ds(band, 2)] = imag_part.astype(jnp.bfloat16).reshape(shape)
        return carry

    strips = pieces * strips_per_piece
    lax.fori_loop(0, strips // 2, unpack, 0)
    relay_step(bands - 1, h_up, h_down, h_side, 1)
    lax.fori_loop(strips // 2, strips, unpack, 0)
    for step in range(2, bands - 1):
        cross_step(step, h_across, 1)
    to_smem = pltpu.make_async_copy(cols_vmem, cols_smem, local_sem.at[0])
    to_smem.start()
    to_smem.wait()

    def block_weights(band, row):
        real = jnp.concatenate([blocks[0, band, row, slot] for slot in range(slots)], axis=1)
        imag = jnp.concatenate([blocks[1, band, row, slot] for slot in range(slots)], axis=1)
        return jnp.concatenate(
            [jnp.concatenate([imag, real], axis=1), jnp.concatenate([-real, imag], axis=1)],
            axis=0,
        )

    def block_rows(band, row, start, count):
        found = []
        for part in range(2):
            for slot in range(slots):
                block = cols_smem[band, row, slot]
                for chunk in range(per_block):
                    place = block * per_block + chunk
                    found.append(
                        current[part, place % pieces, place // pieces, :, pl.ds(start, count)]
                    )
        return jnp.concatenate(found, axis=0)

    def multiply(block, start, count):
        band, row = block // local_blocks, block % local_blocks
        return jnp.dot(
            block_weights(band, row), block_rows(band, row, start, count),
            preferred_element_type=jnp.float32,
        ).astype(jnp.bfloat16)

    def generate(index, carry):
        block = index
        band, row = block // local_blocks, block % local_blocks
        weights = block_weights(band, row)
        span = width * 2
        for start in range(0, order, span):
            product = jnp.dot(
                weights, block_rows(band, row, start, span), preferred_element_type=jnp.float32
            ).astype(jnp.bfloat16)
            for part in range(2):
                for chunk in range(per_block):
                    place = block * per_block + chunk
                    first = part * block_len + chunk * piece_len
                    generator[part, place % pieces, place // pieces, :, pl.ds(start, span)] = (
                        product[first : first + piece_len]
                    )
        return carry

    def combine(factor):
        def body(index, carry):
            start = pl.multiple_of(index * strip, strip)
            owner, band = index // strips_per_piece, index % strips_per_piece * 2
            for part in range(2):
                own = generator[part, owner, pl.ds(band, 2)].reshape(strip, order)
                other = turned(generator.at[part], start)
                own = own.astype(jnp.float32)
                other = other.astype(jnp.float32)
                total = own + other if part == 0 else own - other
                current[part, owner, pl.ds(band, 2)] = (
                    (factor * total).astype(jnp.bfloat16).reshape(2, piece_len, order)
                )
            return carry

        return body

    mine = pl.ds(pl.multiple_of(piece * width, width), width)
    row_ids = z * rows_here + lax.broadcasted_iota(jnp.int32, (rows_here, 1), 0)
    col_place = lax.broadcasted_iota(jnp.int32, (1, width), 1)
    col_band = col_place // piece_len
    col_ids = col_band * rows_here + piece * piece_len + col_place - col_band * piece_len
    upper_mask = row_ids <= col_ids

    def own_rows(ref, part):
        return ref[part, :, z, :, mine].reshape(rows_here, width).astype(jnp.float32)

    def add_own(total):
        return total + jnp.where(upper_mask, own_rows(current, 0), own_rows(current, 1))

    out_ref[...] = jnp.where(upper_mask, own_rows(current, 0), own_rows(current, 1))
    blocks_total = bands * local_blocks
    for term in range(1, TERMS):
        if term == 1:
            lax.fori_loop(z * local_blocks, (z + 1) * local_blocks, generate, 0)
            for position, band in enumerate(others):
                if position == len(others) - 2:
                    cross_step(bands - 1, h_across, 1)
                h_ready(position)
                lax.fori_loop(band * local_blocks, (band + 1) * local_blocks, generate, 0)
        else:
            lax.fori_loop(0, blocks_total, generate, 0)
        lax.fori_loop(0, pieces * strips_per_piece, combine(step_size / term), 0)
        out_ref[...] = add_own(out_ref[...])

    for row in range(local_blocks):
        product = multiply(
            z * local_blocks + row, pl.multiple_of(piece * width, width), width
        )
        for part in range(2):
            for chunk in range(per_block):
                first = part * block_len + chunk * piece_len
                generator[part, row * per_block + chunk, z, :, mine] = (
                    product[first : first + piece_len]
                )
    own_real, own_imag = own_rows(generator, 0), own_rows(generator, 1)
    blocks_per_band = local_blocks

    def own_strip(owner):
        return pl.multiple_of(owner * width + z // 2 * strip, strip)

    def last_rows(index, carry):
        block = index * blocks_per_band + piece // per_block
        half = pl.multiple_of(piece % per_block * piece_len, piece_len)
        band, row = block // local_blocks, block % local_blocks
        rows = pl.ds(half, piece_len)
        real = jnp.concatenate([blocks[0, band, row, t, rows] for t in range(slots)], axis=1)
        imag = jnp.concatenate([blocks[1, band, row, t, rows] for t in range(slots)], axis=1)
        weights = jnp.concatenate(
            [jnp.concatenate([imag, real], axis=1), jnp.concatenate([-real, imag], axis=1)],
            axis=0,
        )
        for pair in range(0, pieces, 2):
            starts = [own_strip(owner) for owner in range(pair, pair + 2)]
            found = [block_rows(band, row, start, strip) for start in starts]
            product = jnp.dot(
                weights, jnp.concatenate(found, axis=1), preferred_element_type=jnp.float32
            ).astype(jnp.bfloat16)
            for side, start in enumerate(starts):
                for part in range(2):
                    generator[part, piece, index, :, pl.ds(start, strip)] = product[
                        part * piece_len : (part + 1) * piece_len,
                        side * strip : (side + 1) * strip,
                    ]
        return carry

    lax.fori_loop(0, bands, last_rows, 0)
    factor = step_size / TERMS
    for owner in range(pieces):
        first = own_strip(owner)
        for part in range(2):
            tall = generator[part, piece, :, :, pl.ds(first, strip)].reshape(width, strip)
            flat = jnp.transpose(tall).astype(jnp.float32)
            flat = jnp.where(z % 2 == 0, flat[:piece_len], flat[piece_len:])
            generator[part, owner, z, :, mine] = flat.astype(jnp.bfloat16)
    real_last = own_real + own_rows(generator, 0)
    imag_last = own_imag - own_rows(generator, 1)
    out_ref[...] = out_ref[...] + factor * jnp.where(upper_mask, real_last, imag_last)

    for part in range(halves):
        for copy in packed_side(z, part):
            copy.wait_send()
        pl.when(has_up)(lambda: packed_up(z, part).wait_send())
        pl.when(has_down)(lambda: packed_down(z, part).wait_send())
        packed_across(z, part).wait_send()
    pl.when(has_up)(lambda: h_up(z, 0).wait_send())
    pl.when(has_down)(lambda: h_down(z, 0).wait_send())
    pl.when(has_up)(lambda: cols_up(z, 0).wait_send())
    pl.when(has_down)(lambda: cols_down(z, 0).wait_send())
    for band in others:
        onward_up = jnp.logical_and(band < z, has_up)
        onward_down = jnp.logical_and(band > z, has_down)
        pl.when(onward_up)(lambda: cols_up(band, 0).wait_send())
        pl.when(onward_down)(lambda: cols_down(band, 0).wait_send())
        for copy in h_side(band, 0):
            copy.wait_send()
        h_across(band, 0).wait_send()
        pl.when(onward_up)(lambda: h_up(band, 0).wait_send())
        pl.when(onward_down)(lambda: h_down(band, 0).wait_send())
        for part in range(halves):
            for copy in packed_side(band, part):
                copy.wait_send()
            packed_across(band, part).wait_send()
            pl.when(onward_up)(lambda: packed_up(band, part).wait_send())
            pl.when(onward_down)(lambda: packed_down(band, part).wait_send())


def gathered_body(packed, h_real, h_imag, h_cols):
    bands, pieces = lax.axis_size("row"), lax.axis_size(("col", "sub"))
    rows_here, width = packed.shape[1], packed.shape[2]
    piece_len = rows_here // pieces
    local_blocks, slots, block_len, _ = h_real.shape
    order = bands * rows_here
    sizes = (bands, pieces, piece_len, block_len, local_blocks, slots)
    out = pl.pallas_call(
        functools.partial(gather_kernel, sizes),
        out_shape=jax.ShapeDtypeStruct((rows_here, width), jnp.float32),
        in_specs=[pl.BlockSpec(memory_space=pl.ANY)] * 4,
        out_specs=pl.BlockSpec(memory_space=pltpu.VMEM),
        scratch_shapes=[
            pltpu.VMEM((pieces, bands, piece_len, order), jnp.bfloat16),
            pltpu.VMEM((2, bands, local_blocks, slots, block_len, block_len), jnp.bfloat16),
            pltpu.VMEM((bands, local_blocks, slots), jnp.int32),
            pltpu.SMEM((bands, local_blocks, slots), jnp.int32),
            pltpu.VMEM((2, pieces, bands, piece_len, order), jnp.bfloat16),
            pltpu.VMEM((2, pieces, bands, piece_len, order), jnp.bfloat16),
            pltpu.SemaphoreType.DMA((5,)),
            pltpu.SemaphoreType.DMA((4, bands, 2)),
            pltpu.SemaphoreType.DMA((bands, 2)),
            pltpu.SemaphoreType.DMA((bands, pieces, 2)),
            pltpu.SemaphoreType.DMA((4, bands, 2)),
            pltpu.SemaphoreType.DMA((bands, 2)),
            pltpu.SemaphoreType.DMA((2, bands, local_blocks, 2)),
            pltpu.SemaphoreType.DMA((2, bands)),
            pltpu.SemaphoreType.DMA((bands,)),
        ],
        compiler_params=pltpu.CompilerParams(collective_id=0, has_side_effects=True),
    )(packed.reshape(pieces, piece_len, width), h_real, h_imag, h_cols)
    return out[None]


def fits(mesh):
    def check(packed, h_real):
        shape = mesh.shape
        bands, pieces = shape["row"], shape["col"] * shape["sub"]
        rows_here = packed.shape[1] // (shape["runs"] * bands)
        piece_len = rows_here // pieces
        order = rows_here * bands
        held = 5 * 2 * order * order
        return (
            shape["col"] == 2 and shape["sub"] == 2 and shape["runs"] == 2
            and bands % 2 == 0 and bands > 2 and packed.shape[2] == bands * piece_len
            and h_real.shape[0] == 2 * bands and h_real.shape[2] == 2 * piece_len
            and 2 * piece_len % 128 == 0 and held < 2**24
        )

    return check


def solution(mesh):
    in_specs = (
        P(("col", "sub"), ("runs", "row"), None),
        P("row", None, None, None),
        P("row", None, None, None),
        P("row", None),
    )
    out_specs = P(("col", "sub"), ("runs", "row"), None)

    def program(packed, h_real, h_imag, h_cols):
        chosen = gathered_body if fits(mesh)(packed, h_real) else body
        return jax.shard_map(
            chosen, mesh=mesh, in_specs=in_specs, out_specs=out_specs, check_vma=False
        )(packed, h_real, h_imag, h_cols)

    return program
```

```python
import functools

import jax
import jax.numpy as jnp
from jax import lax
from jax.experimental import pallas as pl
from jax.experimental.pallas import tpu as pltpu
from jax.sharding import PartitionSpec as P

TERMS = 3


step_size = 0.5


def extended(block, sides, width):
    for axis, dim in sides:
        count = lax.axis_size(axis)
        forward = [(i, i + 1) for i in range(count - 1)]
        forward.append((count - 1, 0))
        backward = [(target, source) for source, target in forward]
        low = lax.ppermute(
            lax.slice_in_dim(block, block.shape[dim] - width, None, axis=dim), axis, forward
        )
        high = lax.ppermute(lax.slice_in_dim(block, 0, width, axis=dim), axis, backward)
        block = jnp.concatenate([low, block, high], axis=dim)
    return block


def mirror(stacked):
    groups, rows_here, col_count = stacked.shape
    piece_count = lax.axis_size(("col", "sub"))
    band_count = lax.axis_size("row")
    piece_len = rows_here // piece_count
    split_rows = stacked.reshape(groups, piece_count, piece_len, col_count)
    arrived = lax.all_to_all(split_rows, ("col", "sub"), split_axis=1, concat_axis=1, tiled=True)
    turned = jnp.swapaxes(arrived.reshape(groups, rows_here, col_count), 1, 2).reshape(
        groups, band_count, piece_len, rows_here
    )
    landed = lax.all_to_all(turned, "row", split_axis=1, concat_axis=1, tiled=True)
    spread = landed.reshape(groups, band_count, piece_len, piece_count, piece_len)
    placed = jnp.transpose(spread, (0, 3, 2, 1, 4))
    return placed.reshape(groups, rows_here, col_count)


def body(packed, h_real, h_imag, h_cols):
    packed_here = packed.reshape(packed.shape[1], packed.shape[2])
    rows_here, col_count = packed_here.shape
    band_index = lax.axis_index("row")
    piece_index = lax.axis_index(("col", "sub"))
    piece_len = rows_here // lax.axis_size(("col", "sub"))
    flipped = mirror(packed_here[None])[0]
    row_ids = band_index * rows_here + jnp.arange(rows_here, dtype=jnp.int32)[:, None]
    col_local = jnp.arange(col_count, dtype=jnp.int32)[None, :]
    col_ids = col_local // piece_len * rows_here + piece_index * piece_len + col_local % piece_len
    upper_mask = row_ids <= col_ids
    real_part = jnp.where(upper_mask, packed_here, flipped)
    imag_part = jnp.where(
        row_ids > col_ids,
        packed_here,
        jnp.where(row_ids < col_ids, -flipped, jnp.zeros_like(flipped)),
    )
    current = jnp.stack([real_part, imag_part])
    summed = current.astype(jnp.float32)
    combined = jnp.stack([jnp.stack([h_imag, h_real], 2), jnp.stack([-h_real, h_imag], 2)])
    local_blocks = h_real.shape[0]
    block_len = h_real.shape[2]
    block_total = lax.axis_size("row") * local_blocks
    block_ids = band_index * local_blocks + jnp.arange(local_blocks, dtype=jnp.int32)[:, None]
    offsets = (h_cols - block_ids + 2) % block_total - 2
    starts = (
        (jnp.arange(local_blocks, dtype=jnp.int32)[:, None] + offsets + 2) * block_len
    ).reshape(-1)
    for term_index in range(1, TERMS + 1):
        padded = extended(current, (("row", 1),), 2 * block_len)
        sliced = jax.vmap(
            lambda row_start: lax.dynamic_slice_in_dim(padded, row_start, block_len, 1)
        )(starts)
        gathered = sliced.reshape(local_blocks, 4, 2, block_len, col_count)
        product = jnp.einsum(
            "obsgij,bsgjc->obic", combined, gathered, preferred_element_type=jnp.float32
        )
        generator = product.reshape(2, rows_here, col_count).astype(jnp.bfloat16)
        mirror_part = mirror(generator).astype(jnp.float32)
        own_part = generator.astype(jnp.float32)
        update = (
            step_size
            / term_index
            * jnp.stack([own_part[0] + mirror_part[0], own_part[1] - mirror_part[1]])
        )
        summed = summed + update
        current = update.astype(jnp.bfloat16)
    result = jnp.where(upper_mask, summed[0], summed[1])
    return result[None]


MESH_ID = pl.DeviceIdType.MESH


def gather_kernel(
    sizes, packed_ref, h_real_ref, h_imag_ref, cols_ref, out_ref,
    whole, blocks, cols_vmem, cols_smem, current, generator, kept_weights, identity,
    local_sem, send_sem, relay_sem, recv_sem, h_send, h_relay, h_recv, cols_send, cols_recv,
):
    bands, pieces, piece_len, block_len, local_blocks, slots = sizes
    rows_here = pieces * piece_len
    width = bands * piece_len
    order = bands * rows_here
    per_block = block_len // piece_len
    strip = 2 * piece_len
    z = lax.axis_index("row")
    x = lax.axis_index("col")
    s = lax.axis_index("sub")
    y = lax.axis_index("runs")
    piece = x * 2 + s
    x_peer, s_peer, y_peer = {"col": 1 - x}, {"sub": 1 - s}, {"runs": 1 - y}

    halves = 2
    half = pieces // halves

    def spot(band, owner, part):
        start = pl.multiple_of(owner * width, width)
        return whole.at[pl.ds(part * half, half), band, :, pl.ds(start, width)]

    def nearest(position):
        inner = jnp.minimum(z, bands - 1 - z)
        sign = 1 if position % 2 == 0 else -1
        beyond = jnp.where(z < bands - 1 - z, z + (position - inner), z - (position - inner))
        return jnp.where(position <= 2 * inner, z + sign * ((position + 1) // 2), beyond)

    others = [nearest(position) for position in range(1, bands)]
    loads = [
        pltpu.make_async_copy(
            packed_ref.at[pl.ds(part * half, half)], spot(z, piece, part), local_sem.at[part]
        )
        for part in range(halves)
    ]
    loads += [
        pltpu.make_async_copy(h_real_ref, blocks.at[0, z], local_sem.at[2]),
        pltpu.make_async_copy(h_imag_ref, blocks.at[1, z], local_sem.at[3]),
        pltpu.make_async_copy(cols_ref, cols_vmem.at[z], local_sem.at[4]),
    ]
    for load in loads:
        load.start()
    identity[...] = jnp.where(
        lax.broadcasted_iota(jnp.int32, (width, width), 0)
        == lax.broadcasted_iota(jnp.int32, (width, width), 1), 1.0, 0.0,
    ).astype(jnp.bfloat16)
    barrier = pltpu.get_barrier_semaphore()
    up, down = {"row": lax.rem(z + 1, bands)}, {"row": lax.rem(z + bands - 1, bands)}
    has_up, has_down = z < bands - 1, z > 0

    def greet(peer):
        pl.semaphore_signal(barrier, 1, device_id=peer, device_id_type=MESH_ID)

    for peer in (s_peer, x_peer, y_peer):
        greet(peer)
    pl.when(has_up)(lambda: greet(up))
    pl.when(has_down)(lambda: greet(down))
    inside = jnp.logical_and(has_up, has_down)
    pl.semaphore_wait(barrier, 3 + jnp.where(inside, 2, 1))

    def send_packed(band, owner, part, sender, peer):
        return pltpu.make_async_remote_copy(
            src_ref=spot(band, owner, part), dst_ref=spot(band, owner, part), send_sem=sender,
            recv_sem=recv_sem.at[band, owner, part], device_id=peer, device_id_type=MESH_ID,
        )

    h_half = slots

    def send_h(kind, band, row, part, sender, peer):
        place = blocks.at[kind, band, row, pl.ds(part * h_half, h_half)]
        return pltpu.make_async_remote_copy(
            src_ref=place, dst_ref=place, send_sem=sender,
            recv_sem=h_recv.at[kind, band, row, part], device_id=peer, device_id_type=MESH_ID,
        )

    def send_cols(band, sender, peer):
        return pltpu.make_async_remote_copy(
            src_ref=cols_vmem.at[band], dst_ref=cols_vmem.at[band], send_sem=sender,
            recv_sem=cols_recv.at[band], device_id=peer, device_id_type=MESH_ID,
        )

    def cols_up(band, part):
        return send_cols(band, cols_send.at[0, band], up)

    def cols_down(band, part):
        return send_cols(band, cols_send.at[1, band], down)

    def no_side(band, part):
        return []

    def packed_up(band, part):
        return send_packed(band, piece, part, send_sem.at[0, band, part], up)

    def packed_down(band, part):
        return send_packed(band, piece, part, send_sem.at[1, band, part], down)

    def packed_side(band, part):
        return [send_packed(band, piece, part, send_sem.at[2, band, part], x_peer),
                send_packed(band, piece, part, send_sem.at[3, band, part], s_peer)]

    def packed_across(band, part):
        return send_packed(band, (1 - x) * 2 + s, part, relay_sem.at[band, part], s_peer)

    def h_up(band, part):
        return send_h(y, band, s, part, h_send.at[0, band, part], up)

    def h_down(band, part):
        return send_h(y, band, s, part, h_send.at[1, band, part], down)

    def h_side(band, part):
        return [send_h(y, band, s, part, h_send.at[2, band, part], y_peer),
                send_h(y, band, s, part, h_send.at[3, band, part], s_peer)]

    def h_across(band, part):
        return send_h(1 - y, band, s, part, h_relay.at[band, part], s_peer)

    def start_all(copies):
        for copy in copies:
            copy.start()

    def pass_on(copy):
        copy.wait_recv()
        copy.start()

    for part in range(halves):
        loads[part].wait()
        pl.when(has_up)(lambda: packed_up(z, part).start())
        pl.when(has_down)(lambda: packed_down(z, part).start())
        start_all(packed_side(z, part))
    for load in loads[halves:]:
        load.wait()
    pl.when(has_up)(lambda: cols_up(z, 0).start())
    pl.when(has_down)(lambda: cols_down(z, 0).start())

    def begin_h(step):
        up_at = jnp.where(z == bands - 2, 0, z)
        down_at = jnp.where(z == 1, 0, bands - 1 - z)
        now_up = jnp.logical_and(up_at == step, has_up)
        now_down = jnp.logical_and(down_at == step, has_down)
        pl.when(now_up)(lambda: h_up(z, 0).start())
        pl.when(now_down)(lambda: h_down(z, 0).start())

    begin_h(0)

    def relay_step(step, make_up, make_down, make_side, count):
        below, above = z - step, z + step
        for part in range(count):
            @pl.when(below >= 0)
            def _():
                make_up(below, part).wait_recv()
                pl.when(has_up)(lambda: make_up(below, part).start())
                start_all(make_side(below, part))

            @pl.when(above < bands)
            def _():
                make_down(above, part).wait_recv()
                pl.when(has_down)(lambda: make_down(above, part).start())
                start_all(make_side(above, part))

    def cross_step(step, make_across, count):
        for part in range(count):
            pl.when(z - step >= 0)(lambda: pass_on(make_across(z - step, part)))
            pl.when(z + step < bands)(lambda: pass_on(make_across(z + step, part)))

    def h_ready(position):
        for kind in range(2):
            for part in range(1):
                send_h(
                    kind, others[position], 1 - s, part, h_relay.at[0, 0], s_peer
                ).wait_recv()

    pairs = bands // 2
    own_pair = z // 2

    def within_pair(place):
        return place // piece_len * rows_here + place % piece_len

    base_gap = within_pair(lax.broadcasted_iota(jnp.int32, (strip, 1), 0)) - within_pair(
        lax.broadcasted_iota(jnp.int32, (1, strip), 1)
    )

    def strip_at(owner, pair):
        return pl.multiple_of(owner * width + pair * strip, strip)

    def tile(ref, owner, pair, start):
        return ref[owner, pl.ds(pair * 2, 2), :, pl.ds(start, strip)].reshape(strip, strip)

    def place_tile(part, owner, pair, start, value):
        current[part, owner, pl.ds(pair * 2, 2), :, pl.ds(start, strip)] = (
            value.astype(jnp.bfloat16).reshape(2, piece_len, strip)
        )

    def unpack_same(pair):
        def body(owner, carry):
            start = strip_at(owner, pair)
            for other in range(pieces):
                there = strip_at(other, pair)
                here = tile(whole, owner, pair, there).astype(jnp.float32)
                flipped = jnp.transpose(tile(whole, other, pair, start)).astype(jnp.float32)
                gap = base_gap + (owner - other) * piece_len
                place_tile(0, owner, pair, there, jnp.where(gap <= 0, here, flipped))
                place_tile(
                    1, owner, pair, there,
                    jnp.where(gap > 0, here, jnp.where(gap < 0, -flipped, 0.0)),
                )
            return carry

        lax.fori_loop(0, pieces, body, 0)

    def unpack_apart(low, high):
        def body(owner, carry):
            start = strip_at(owner, low)
            for other in range(pieces):
                there = strip_at(other, high)
                upper = tile(whole, owner, low, there)
                lower = tile(whole, other, high, start)
                place_tile(0, owner, low, there, upper)
                place_tile(1, other, high, start, lower)
                place_tile(0, other, high, start, jnp.transpose(upper))
                place_tile(1, owner, low, there, -jnp.transpose(lower))
            return carry

        lax.fori_loop(0, pieces, body, 0)

    def packed_ready(band):
        for owner in (x * 2 + (1 - s), (1 - x) * 2 + (1 - s)):
            for part in range(halves):
                send_packed(band, owner, part, relay_sem.at[band, part], s_peer).wait_recv()

    outside = jnp.logical_not(inside)
    relay_step(1, packed_up, packed_down, packed_side, halves)
    begin_h(1)
    for part in range(halves):
        pass_on(packed_across(z, part))
    pl.when(outside)(lambda: relay_step(1, h_up, h_down, h_side, 1))
    relay_step(2, packed_up, packed_down, packed_side, halves)
    begin_h(2)
    cross_step(1, packed_across, halves)
    relay_step(1, cols_up, cols_down, no_side, 1)
    pl.when(inside)(lambda: relay_step(1, h_up, h_down, h_side, 1))
    for step in range(3, bands):
        relay_step(step, packed_up, packed_down, packed_side, halves)
        begin_h(step)
    for step in range(2, bands - 1):
        cross_step(step, packed_across, halves)
        relay_step(step, cols_up, cols_down, no_side, 1)
    packed_ready(own_pair * 2)
    packed_ready(own_pair * 2 + 1)
    unpack_same(own_pair)
    cross_step(bands - 1, packed_across, halves)
    relay_step(bands - 1, cols_up, cols_down, no_side, 1)
    to_smem = pltpu.make_async_copy(cols_vmem, cols_smem, local_sem.at[0])
    to_smem.start()
    for step in range(2, bands - 1):
        relay_step(step, h_up, h_down, h_side, 1)
    cross_step(1, h_across, 1)
    for step in range(1, pairs):
        later = lax.rem(own_pair + step, pairs)
        packed_ready(later * 2)
        packed_ready(later * 2 + 1)
    for low in range(pairs):
        for high in range(low + 1, pairs):
            unpack_apart(low, high)
    relay_step(bands - 1, h_up, h_down, h_side, 1)
    for step in range(1, pairs):
        unpack_same(lax.rem(own_pair + step, pairs))
    to_smem.wait()
    def block_weights(band, row):
        real = jnp.concatenate([blocks[0, band, row, slot] for slot in range(slots)], axis=1)
        imag = jnp.concatenate([blocks[1, band, row, slot] for slot in range(slots)], axis=1)
        return jnp.concatenate(
            [jnp.concatenate([imag, real], axis=1), jnp.concatenate([-real, imag], axis=1)],
            axis=0,
        )

    def block_rows(band, row, start, count):
        found = []
        for part in range(2):
            for slot in range(slots):
                block = cols_smem[band, row, slot]
                for chunk in range(per_block):
                    place = block * per_block + chunk
                    found.append(
                        current[part, place % pieces, place // pieces, :, pl.ds(start, count)]
                    )
        return jnp.concatenate(found, axis=0)

    def multiply(block, start, count):
        band, row = block // local_blocks, block % local_blocks
        return jnp.dot(
            block_weights(band, row), block_rows(band, row, start, count),
            preferred_element_type=jnp.float32,
        ).astype(jnp.bfloat16)

    span = order // 2

    def generate(term, band):
        for row in range(local_blocks):
            if term == 1:
                kept_weights[band, row] = block_weights(band, row)
            for start in range(0, order, span):
                product = jnp.dot(
                    kept_weights[band, row], block_rows(band, row, start, span),
                    preferred_element_type=jnp.float32,
                ).astype(jnp.bfloat16)
                for part in range(2):
                    for chunk in range(per_block):
                        first = part * block_len + chunk * piece_len
                        generator[part, row * per_block + chunk, band, :, pl.ds(start, span)] = (
                            product[first : first + piece_len]
                        )

    mine = pl.ds(pl.multiple_of(piece * width, width), width)

    def flip(tall):
        return lax.dot_general(
            identity[...], tall, (((1,), (1,)), ((), ())), preferred_element_type=jnp.float32
        )

    def joined(own, tall, part, factor):
        mirrored = flip(tall)
        own = own.astype(jnp.float32)
        total = own + mirrored if part == 0 else own - mirrored
        return (factor * total).astype(jnp.bfloat16)

    def combine_all(factor):
        def body(owner, carry):
            lanes = pl.ds(pl.multiple_of(owner * width, width), width)
            for part in range(2):
                own = generator[part, owner].reshape(width, order)
                tall = generator[part, :, :, :, lanes].reshape(order, width)
                total = joined(own, tall, part, factor)
                current[part, owner] = total.reshape(bands, piece_len, order)
            return carry

        lax.fori_loop(0, pieces, body, 0, unroll=True)

    row_ids = z * rows_here + lax.broadcasted_iota(jnp.int32, (rows_here, 1), 0)
    col_place = lax.broadcasted_iota(jnp.int32, (1, width), 1)
    col_band = col_place // piece_len
    col_ids = col_band * rows_here + piece * piece_len + col_place - col_band * piece_len
    upper_mask = row_ids <= col_ids

    def own_rows(ref, part):
        return ref[part, :, z, :, mine].reshape(rows_here, width).astype(jnp.float32)

    def add_own(total):
        return total + jnp.where(upper_mask, own_rows(current, 0), own_rows(current, 1))

    out_ref[...] = jnp.where(upper_mask, own_rows(current, 0), own_rows(current, 1))
    for term in range(1, TERMS):
        generate(term, z)
        for position, band in enumerate(others):
            if term == 1:
                if position < bands - 2:
                    cross_step(position + 2, h_across, 1)
                h_ready(position)
            generate(term, band)
        combine_all(step_size / term)
        out_ref[...] = add_own(out_ref[...])
    for row in range(local_blocks):
        product = multiply(
            z * local_blocks + row, pl.multiple_of(piece * width, width), width
        )
        for part in range(2):
            for chunk in range(per_block):
                first = part * block_len + chunk * piece_len
                generator[part, row * per_block + chunk, z, :, mine] = (
                    product[first : first + piece_len]
                )
    own_real, own_imag = own_rows(generator, 0), own_rows(generator, 1)

    def own_strip(owner):
        return strip_at(owner, own_pair)

    row = piece // per_block
    offset = pl.multiple_of(piece % per_block * piece_len, piece_len)
    for band in range(bands):
        weights = jnp.concatenate(
            [kept_weights[band, row, pl.ds(part * block_len + offset, piece_len)] for part in range(2)],
            axis=0,
        )
        found = [block_rows(band, row, own_strip(owner), strip) for owner in range(pieces)]
        product = jnp.dot(
            weights, jnp.concatenate(found, axis=1), preferred_element_type=jnp.float32
        ).astype(jnp.bfloat16)
        for owner in range(pieces):
            for part in range(2):
                generator[part, piece, band, :, pl.ds(own_strip(owner), strip)] = product[
                    part * piece_len : (part + 1) * piece_len, owner * strip : (owner + 1) * strip
                ]
    factor = step_size / TERMS
    for owner in range(pieces):
        first = own_strip(owner)
        for part in range(2):
            tall = generator[part, piece, :, :, pl.ds(first, strip)].reshape(width, strip)
            flat = jnp.transpose(tall).astype(jnp.float32)
            flat = jnp.where(z % 2 == 0, flat[:piece_len], flat[piece_len:])
            generator[part, owner, z, :, mine] = flat.astype(jnp.bfloat16)
    real_last = own_real + own_rows(generator, 0)
    imag_last = own_imag - own_rows(generator, 1)
    out_ref[...] = out_ref[...] + factor * jnp.where(upper_mask, real_last, imag_last)

    for part in range(halves):
        for copy in packed_side(z, part):
            copy.wait_send()
        pl.when(has_up)(lambda: packed_up(z, part).wait_send())
        pl.when(has_down)(lambda: packed_down(z, part).wait_send())
        packed_across(z, part).wait_send()
    pl.when(has_up)(lambda: h_up(z, 0).wait_send())
    pl.when(has_down)(lambda: h_down(z, 0).wait_send())
    pl.when(has_up)(lambda: cols_up(z, 0).wait_send())
    pl.when(has_down)(lambda: cols_down(z, 0).wait_send())
    for band in others:
        onward_up = jnp.logical_and(band < z, has_up)
        onward_down = jnp.logical_and(band > z, has_down)
        pl.when(onward_up)(lambda: cols_up(band, 0).wait_send())
        pl.when(onward_down)(lambda: cols_down(band, 0).wait_send())
        for copy in h_side(band, 0):
            copy.wait_send()
        h_across(band, 0).wait_send()
        pl.when(onward_up)(lambda: h_up(band, 0).wait_send())
        pl.when(onward_down)(lambda: h_down(band, 0).wait_send())
        for part in range(halves):
            for copy in packed_side(band, part):
                copy.wait_send()
            packed_across(band, part).wait_send()
            pl.when(onward_up)(lambda: packed_up(band, part).wait_send())
            pl.when(onward_down)(lambda: packed_down(band, part).wait_send())


def gathered_body(packed, h_real, h_imag, h_cols):
    bands, pieces = lax.axis_size("row"), lax.axis_size(("col", "sub"))
    rows_here, width = packed.shape[1], packed.shape[2]
    piece_len = rows_here // pieces
    local_blocks, slots, block_len, _ = h_real.shape
    order = bands * rows_here
    sizes = (bands, pieces, piece_len, block_len, local_blocks, slots)
    out = pl.pallas_call(
        functools.partial(gather_kernel, sizes),
        out_shape=jax.ShapeDtypeStruct((rows_here, width), jnp.float32),
        in_specs=[pl.BlockSpec(memory_space=pl.ANY)] * 4,
        out_specs=pl.BlockSpec(memory_space=pltpu.VMEM),
        scratch_shapes=[
            pltpu.VMEM((pieces, bands, piece_len, order), jnp.bfloat16),
            pltpu.VMEM((2, bands, local_blocks, slots, block_len, block_len), jnp.bfloat16),
            pltpu.VMEM((bands, local_blocks, slots), jnp.int32),
            pltpu.SMEM((bands, local_blocks, slots), jnp.int32),
            pltpu.VMEM((2, pieces, bands, piece_len, order), jnp.bfloat16),
            pltpu.VMEM((2, pieces, bands, piece_len, order), jnp.bfloat16),
            pltpu.VMEM(
                (bands, local_blocks, 2 * block_len, 2 * slots * block_len), jnp.bfloat16
            ),
            pltpu.VMEM((width, width), jnp.bfloat16),
            pltpu.SemaphoreType.DMA((5,)),
            pltpu.SemaphoreType.DMA((4, bands, 2)),
            pltpu.SemaphoreType.DMA((bands, 2)),
            pltpu.SemaphoreType.DMA((bands, pieces, 2)),
            pltpu.SemaphoreType.DMA((4, bands, 2)),
            pltpu.SemaphoreType.DMA((bands, 2)),
            pltpu.SemaphoreType.DMA((2, bands, local_blocks, 2)),
            pltpu.SemaphoreType.DMA((2, bands)),
            pltpu.SemaphoreType.DMA((bands,)),
        ],
        compiler_params=pltpu.CompilerParams(collective_id=0, has_side_effects=True),
    )(packed.reshape(pieces, piece_len, width), h_real, h_imag, h_cols)
    return out[None]


def fits(mesh):
    def check(packed, h_real):
        shape = mesh.shape
        bands, pieces = shape["row"], shape["col"] * shape["sub"]
        rows_here = packed.shape[1] // (shape["runs"] * bands)
        piece_len = rows_here // pieces
        order = rows_here * bands
        held = 5 * 2 * order * order
        return (
            shape["col"] == 2 and shape["sub"] == 2 and shape["runs"] == 2
            and bands % 2 == 0 and bands > 2 and packed.shape[2] == bands * piece_len
            and h_real.shape[0] == 2 * bands and h_real.shape[2] == 2 * piece_len
            and 2 * piece_len % 128 == 0 and held < 2**24
        )

    return check


def solution(mesh):
    in_specs = (
        P(("col", "sub"), ("runs", "row"), None),
        P("row", None, None, None),
        P("row", None, None, None),
        P("row", None),
    )
    out_specs = P(("col", "sub"), ("runs", "row"), None)

    def program(packed, h_real, h_imag, h_cols):
        chosen = gathered_body if fits(mesh)(packed, h_real) else body
        return jax.shard_map(
            chosen, mesh=mesh, in_specs=in_specs, out_specs=out_specs, check_vma=False
        )(packed, h_real, h_imag, h_cols)

    return program
```
